32 devices in a mesh: space: 16 (over z, x, core), chan: 2 (over y).
Axes of the slice: x: 2, y: 2, z: 4, core: 2. Of those that a mesh axis runs over, the one named last changes fastest.
Arguments:
- state: bfloat16 [96, 512, 1024], P('space', 'chan'), may hold values from -6 to 6
- cotangent: bfloat16 [96, 512, 1024], P('space', None, 'chan'), may hold values from -6 to 6
- order_table: int32 [96], replicated, may hold values from 0 to 95, as said below
- quad_weight: float32 [96], P('space'), may hold values from 0.5 to 2
- legendre: bfloat16 [96, 96, 96], P('space', 'chan'), as said below
- spec_gain: float32 [96, 512], P('chan'), may hold values from 0.5 to 2
- spectral_weight: bfloat16 [2, 512, 512], replicated, may hold values from -0.1875 to 0.1875
- mlp_in: bfloat16 [512, 768], P('chan'), may hold values from -0.25 to 0.25
- mlp_out: bfloat16 [768, 512], P('chan'), may hold values from -0.21875 to 0.21875
Outputs:
- output: bfloat16 [96, 512, 1024], P('space', None, 'chan')
- state_grad: bfloat16 [96, 512, 1024], P('space', 'chan')
The draws below stay inside these ranges and needn't reach their ends.
Inputs may be any that keep to these rules, and one draw needn't show every extreme that they name: order_table holds each of 0 to 95 once; slots 2 j and 2 j + 1 hold orders m and 95 - m with m < 48. legendre[k, l, t] is zero for every degree l below order_table[k].
All inputs are finite; a program needn't handle non-finite values.
Results may differ from the reference program's by a relative error of at most 0.015.
Values may be sent and summed in bfloat16 or wider, within the bound.
A program may use at most 64 MiB of HBM per device.

```python
import math
import jax
import jax.numpy as jnp
from jax import lax

C = 512
H = 768
NLON = 1024
NLAT = 96
M = 96


def pairing(key):
    shuffled = jax.random.permutation(jax.random.fold_in(key, 11), M // 2).astype(jnp.int32)
    return jnp.stack([shuffled, M - 1 - shuffled], axis=1).reshape(M).astype(jnp.int32)


def draw_order_table(key, part):
    return pairing(key)


def draw_legendre(key, part):
    orders = pairing(key)
    degree = lax.broadcasted_iota(jnp.int32, (M, M, NLAT), 1)
    live = degree >= orders[:, None, None]
    value_key = jax.random.fold_in(key, 23)
    values = jax.random.normal(value_key, (M, M, NLAT), jnp.float32)
    scaled = jnp.where(live, values, 0.0) * (1.0 / NLAT) ** 0.5
    return scaled.astype(jnp.bfloat16)


def block_levels(own_key, shape, cuts, low, high):
    def one(position, parts):
        draws = jax.random.uniform(jax.random.fold_in(jax.random.fold_in(own_key, 6), position), (parts,), jnp.float32, low / len(cuts), high / len(cuts))
        return jnp.repeat(jnp.exp(draws), shape[position] // parts).reshape((-1,) + (1,) * (len(shape) - position - 1))

    loudness = one(*cuts[0])
    for cut in cuts[1:]:
        loudness = loudness * one(*cut)
    return loudness


def scatter_about(key, shape, width, limit, shards=(), held_as=jnp.bfloat16):
    result = jax.random.normal(key, shape, jnp.float32) * width
    if len(shards) > 0:
        result = block_levels(key, shape, shards, -0.22, 0.18) * result
    return jnp.clip(result, min=-limit, max=limit).astype(held_as)


def setup_inputs(seed: int = 0) -> dict:
    splits = jax.random.split(jax.random.key(seed), 10)
    return {
        "state": scatter_about(splits[0], (NLAT, C, NLON), 1.0, 6.0, ((0, 16), (1, 2))),
        "cotangent": scatter_about(splits[1], (NLAT, C, NLON), 1.0, 6.0, ((0, 16), (2, 2))),
        "order_table": draw_order_table(jax.random.fold_in(splits[9], 71), 0),
        "quad_weight": jnp.clip(jnp.exp(math.log(2.0) - 1.3862944 * jax.random.uniform(splits[3], (NLAT,), jnp.float32) ** block_levels(splits[3], (NLAT,), ((0, 16),), -0.2, 0.2)), 0.5, 2.0),
        "legendre": draw_legendre(jax.random.fold_in(splits[9], 71), 0),
        "spec_gain": jnp.clip(jnp.exp(math.log(2.0) - 1.3862944 * jax.random.uniform(splits[5], (M, C), jnp.float32) ** block_levels(splits[5], (M, C), ((0, 2),), -0.2, 0.2)), 0.5, 2.0),
        "spectral_weight": scatter_about(splits[6], (2, C, C), (2 * C) ** -0.5, 0.1875),
        "mlp_in": scatter_about(splits[7], (C, H), C ** -0.5, 0.25, ((0, 2),)),
        "mlp_out": scatter_about(splits[8], (H, C), H ** -0.5, 0.21875, ((0, 2),)),
    }


def transform_tables(order_table, lon_count):
    points = lax.broadcasted_iota(jnp.int32, (lon_count, order_table.shape[0]), 0)
    phases = points * order_table.astype(jnp.int32)[None, :] % lon_count
    angles = phases.astype(jnp.float32) * (2.0 * math.pi / lon_count)
    factor = 1.0 / math.sqrt(lon_count)
    forward = jnp.stack([jnp.cos(angles), -jnp.sin(angles)], axis=2) * factor
    weighting = jnp.where(order_table == 0, 1.0, 2.0).astype(jnp.float32)
    inverse = forward * weighting[None, :, None]
    return (forward.reshape(lon_count, -1).astype(jnp.bfloat16), inverse.reshape(lon_count, -1).astype(jnp.bfloat16))

def rounded(values):
    return lax.optimization_barrier(values.astype(jnp.bfloat16))

def mlp_row(row_pair, mlp_in, mlp_out):
    hidden_row, cot_row = row_pair
    first_layer = mlp_in.astype(jnp.float32)
    second_layer = mlp_out.astype(jnp.float32)
    pre_act = jnp.einsum('cn,ch->hn', hidden_row.astype(jnp.float32), first_layer)
    active = rounded(jax.nn.gelu(pre_act)).astype(jnp.float32)
    output_row = (hidden_row.astype(jnp.float32) + jnp.einsum('hn,hc->cn', active, second_layer)).astype(jnp.bfloat16)
    back_hidden = jnp.einsum('cn,hc->hn', cot_row.astype(jnp.float32), second_layer)
    pullback = jax.vjp(jax.nn.gelu, pre_act)[1]
    inner_grad = rounded(pullback(back_hidden)[0]).astype(jnp.float32)
    grad_row = (cot_row.astype(jnp.float32) + jnp.einsum('hn,ch->cn', inner_grad, first_layer)).astype(jnp.bfloat16)
    return (output_row, grad_row)

def reference(state, cotangent, order_table, quad_weight, legendre, spec_gain, spectral_weight, mlp_in, mlp_out):
    forward_table, inverse_table = transform_tables(order_table, NLON)
    forward_grid = forward_table.astype(jnp.float32).reshape(NLON, M, 2)
    inverse_grid = inverse_table.astype(jnp.float32).reshape(NLON, M, 2)
    legend = legendre.astype(jnp.float32)
    weight_real = spectral_weight[0].astype(jnp.float32)
    weight_imag = spectral_weight[1].astype(jnp.float32)
    gains = spec_gain[:, None, :]
    spectral = rounded(jnp.einsum('tcn,nkr->tkrc', state.astype(jnp.float32), forward_grid) * quad_weight[:, None, None, None])
    coeffs = rounded(jnp.einsum('klt,tkrc->lkrc', legend, spectral.astype(jnp.float32)))
    coeff_real = coeffs[:, :, 0].astype(jnp.float32)
    coeff_imag = coeffs[:, :, 1].astype(jnp.float32)
    mixed_real = (jnp.einsum('lkc,co->lko', coeff_real, weight_real) - jnp.einsum('lkc,co->lko', coeff_imag, weight_imag)) * gains
    mixed_imag = (jnp.einsum('lkc,co->lko', coeff_real, weight_imag) + jnp.einsum('lkc,co->lko', coeff_imag, weight_real)) * gains
    mixed = rounded(jnp.stack([mixed_real, mixed_imag], axis=2))
    synth = rounded(jnp.einsum('klt,lkrc->tkrc', legend, mixed.astype(jnp.float32)))
    wave = jnp.einsum('tkrc,nkr->tcn', synth.astype(jnp.float32), inverse_grid)
    hidden = rounded(state.astype(jnp.float32) + wave)
    output, hidden_grad = lax.map(lambda row_pair: mlp_row(row_pair, mlp_in, mlp_out), (hidden, cotangent))
    back_spec = rounded(jnp.einsum('tcn,nkr->tkrc', hidden_grad.astype(jnp.float32), inverse_grid))
    back_coeff = rounded(jnp.einsum('klt,tkrc->lkrc', legend, back_spec.astype(jnp.float32)))
    scaled_real = rounded(back_coeff[:, :, 0].astype(jnp.float32) * gains).astype(jnp.float32)
    scaled_imag = rounded(back_coeff[:, :, 1].astype(jnp.float32) * gains).astype(jnp.float32)
    back_real = jnp.einsum('lko,co->lkc', scaled_real, weight_real) + jnp.einsum('lko,co->lkc', scaled_imag, weight_imag)
    back_imag = jnp.einsum('lko,co->lkc', scaled_imag, weight_real) - jnp.einsum('lko,co->lkc', scaled_real, weight_imag)
    back_mixed = rounded(jnp.stack([back_real, back_imag], axis=2))
    back_field = rounded(jnp.einsum('klt,lkrc->tkrc', legend, back_mixed.astype(jnp.float32)))
    field_grad = jnp.einsum('tkrc,nkr->tcn', back_field.astype(jnp.float32), forward_grid) * quad_weight[:, None, None]
    state_grad = (hidden_grad.astype(jnp.float32) + field_grad).astype(jnp.bfloat16)
    return (output, state_grad)
```

```python
import functools
import math

import jax
import jax.numpy as jnp
from jax import lax
from jax.experimental import pallas as pl
from jax.experimental.pallas import tpu as pltpu
from jax.sharding import PartitionSpec as P

BF = jnp.bfloat16
F32 = jnp.float32
BOTH = ("space", "chan")
ROOT = math.sqrt(2.0 / math.pi)


def transform_table(order_table, lon_count):
    points = lax.broadcasted_iota(jnp.int32, (lon_count, 2 * order_table.shape[0]), 0)
    column = lax.broadcasted_iota(jnp.int32, (lon_count, 2 * order_table.shape[0]), 1)
    phases = points * jnp.repeat(order_table, 2)[None, :] % lon_count
    angles = phases.astype(F32) * (2.0 * math.pi / lon_count)
    waves = jnp.where(column % 2 == 0, jnp.cos(angles), -jnp.sin(angles))
    return (waves * (1.0 / math.sqrt(lon_count))).astype(BF)


def chan_swap(values, split_axis, concat_axis):
    count = lax.axis_size("chan")
    me = lax.axis_index("chan")
    width = values.shape[split_axis] // count
    depth = values.shape[concat_axis]
    shape = list(values.shape)
    shape[split_axis] = width
    shape[concat_axis] = depth * count
    result = jnp.zeros(shape, values.dtype)
    for shift in range(count):
        piece = lax.dynamic_slice_in_dim(values, (me + shift) % count * width, width, split_axis)
        if shift:
            ring = [(i, (i + shift) % count) for i in range(count)]
            piece = lax.ppermute(piece, "chan", ring)
        source = (me - shift + count) % count
        result = lax.dynamic_update_slice_in_dim(result, piece, source * depth, concat_axis)
    return result


def chan_rows(values, share):
    count = lax.axis_size("chan")
    me = lax.axis_index("chan")
    rows = values.shape[0]
    result = jnp.zeros((rows * count,) + values.shape[1:], values.dtype)
    result = lax.dynamic_update_slice_in_dim(result, values, me * rows, 0)
    space = lax.axis_size("space")
    share = share and space % 2 == 0
    parity = lax.axis_index("space") % 2
    part = rows // 2 if share else rows
    mine = lax.dynamic_slice_in_dim(values, parity * part, part, 0) if share else values
    for shift in range(1, count):
        ring = [(i, (i + shift) % count) for i in range(count)]
        source = (me - shift + count) % count
        piece = lax.ppermute(mine, "chan", ring)
        if share:
            other = lax.ppermute(piece, "space", [(i, i ^ 1) for i in range(space)])
            result = lax.dynamic_update_slice_in_dim(
                result, piece, source * rows + parity * part, 0
            )
            result = lax.dynamic_update_slice_in_dim(
                result, other, source * rows + (1 - parity) * part, 0
            )
        else:
            result = lax.dynamic_update_slice_in_dim(result, piece, source * rows, 0)
    return result


def dot(left, right, dims):
    return lax.dot_general(left, right, (dims, ((), ())), preferred_element_type=F32)


def mlp_kernel(state, cot, synth, table, first, first_t, second, second_t, out, grad, spec):
    grid_table = table[...]
    wave = dot(synth[0], grid_table, ((0,), (0,)))
    hidden = (state[0].astype(F32) + wave).astype(BF)
    pre = dot(first_t[...], hidden, ((1,), (0,)))
    square = pre * pre
    curve = jnp.tanh(ROOT * (pre + 0.044715 * (square * pre)))
    half = 0.5 * (1.0 + curve)
    active = (pre * half).astype(BF)
    out[0] = (hidden.astype(F32) + dot(second_t[...], active, ((1,), (0,)))).astype(BF)
    slope = half + 0.5 * pre * (1.0 - curve * curve) * (ROOT * (1.0 + 0.134145 * square))
    inner = (slope * dot(second[...], cot[0], ((1,), (0,)))).astype(BF)
    back = (cot[0].astype(F32) + dot(first[...], inner, ((1,), (0,)))).astype(BF)
    grad[0] = back
    spec[0] = dot(grid_table, back, ((1,), (1,))).astype(BF)


def mlp(state, cot, synth, table, first, second):
    lats, chans, lons = state.shape
    waves = synth.shape[1]
    hidden = first.shape[1]

    def whole(*shape):
        return pl.BlockSpec(shape, lambda t: (0,) * len(shape))

    def row(*shape):
        return pl.BlockSpec((1,) + shape, lambda t: (t, 0, 0))

    return pl.pallas_call(
        mlp_kernel,
        grid=(lats,),
        in_specs=[
            row(chans, lons),
            row(chans, lons),
            row(waves, chans),
            whole(waves, lons),
            whole(chans, hidden),
            whole(hidden, chans),
            whole(hidden, chans),
            whole(chans, hidden),
        ],
        out_specs=[row(chans, lons), row(chans, lons), row(waves, chans)],
        out_shape=[
            jax.ShapeDtypeStruct((lats, chans, lons), BF),
            jax.ShapeDtypeStruct((lats, chans, lons), BF),
            jax.ShapeDtypeStruct((lats, waves, chans), BF),
        ],
        compiler_params=pltpu.CompilerParams(vmem_limit_bytes=56 << 20),
    )(state, cot, synth, table, first, first.T, second, second.T)


def einsum(form, *values):
    return jnp.einsum(form, *values, preferred_element_type=F32)


def spread_paths(legendre, spec_gain, weights, lats, chan_width):
    spaces, chans = lax.axis_size("space"), lax.axis_size("chan")
    devices = spaces * chans
    table = chan_swap(legendre, 0, 1)
    slots, degrees, lat_count = table.shape
    gains = chan_rows(spec_gain, False)
    real, imag = weights[0], weights[1]
    channels = real.shape[0]
    by_shard = (chans, 1, chan_width, 2 * channels)
    top = jnp.concatenate([real, imag], axis=1).reshape(by_shard)
    low = jnp.concatenate([-imag, real], axis=1).reshape(by_shard)
    mixer = jnp.concatenate([top, low], axis=1).reshape(2 * channels, 2 * channels)
    table_st = table.reshape(slots, degrees, spaces, lats)

    def swap(values):
        return lax.all_to_all(values, BOTH, 0, 0, tiled=True)

    def forward(spectral):
        sent = spectral.reshape(lats, devices, 2 * slots, chan_width).transpose(1, 0, 2, 3)
        got = swap(sent).reshape(spaces, chans, lats, slots, 2, chan_width)
        coeffs = einsum("klst,sytkrc->klyrc", table_st, got).astype(BF)
        coeffs = coeffs.reshape(slots, degrees, 2 * channels)
        mixed = einsum("klx,xo->klo", coeffs, mixer).reshape(slots, degrees, 2, channels)
        mixed = (mixed * gains[None, :, None, :]).astype(BF)
        synth = einsum("klst,klro->sktro", table_st, mixed).astype(BF)
        synth = jnp.broadcast_to(synth[:, None], (spaces, chans) + synth.shape[1:])
        got = swap(synth.reshape((devices, slots) + (lats, 2 * channels)))
        return (
            got.reshape(devices, slots, lats, 2, channels)
            .transpose(2, 0, 1, 3, 4)
            .reshape(lats, devices * slots * 2, channels)
        )

    def backward(part):
        sent = part.reshape(lats, devices, 2 * slots, channels).transpose(1, 0, 2, 3)
        got = swap(sent).reshape(spaces, chans, lats, slots, 2, channels)
        table_sy = jnp.broadcast_to(
            table_st[:, :, :, None], (slots, degrees, spaces, chans, lats)
        )
        coeffs = einsum("klsyt,sytkro->klro", table_sy, got).astype(BF)
        scaled = (coeffs.astype(F32) * gains[None, :, None, :]).astype(BF)
        scaled = scaled.reshape(slots, degrees, 2 * channels)
        mixed = einsum("klo,xo->klx", scaled, mixer).astype(BF)
        mixed = mixed.reshape(slots, degrees, chans, 2, chan_width)
        field = einsum("klst,klyrc->syktrc", table_st, mixed).astype(BF)
        got = swap(field.reshape((devices, slots, lats, 2 * chan_width)))
        return (
            got.reshape(devices, slots, lats, 2, chan_width)
            .transpose(2, 0, 1, 3, 4)
            .reshape(lats, devices * slots * 2, chan_width)
        )

    return forward, backward


def shard_paths(legendre, spec_gain, weights, lats, chan_width):
    chans = lax.axis_size("chan")
    table = lax.all_gather(legendre, "chan", axis=1, tiled=True)
    slots = table.shape[0]
    channels = weights.shape[1]

    def to_orders(values):
        return lax.all_to_all(values, "space", split_axis=1, concat_axis=0, tiled=True)

    def to_bands(values):
        return lax.all_to_all(values, "space", split_axis=0, concat_axis=1, tiled=True)

    def to_degrees(values):
        return lax.all_to_all(values, "chan", split_axis=0, concat_axis=3, tiled=True)

    def to_channels(values):
        return lax.all_to_all(values, "chan", split_axis=3, concat_axis=0, tiled=True)

    def analysis(spectral):
        values = spectral.reshape(lats, -1, 2, chan_width)
        coeffs = einsum("klt,tkrc->lkrc", table, to_orders(values)).astype(BF)
        return to_degrees(coeffs)

    def synthesis(mixed):
        field = einsum("klt,lkrc->tkrc", table, to_channels(mixed.astype(BF))).astype(BF)
        return to_bands(field).reshape(lats, -1, chan_width)

    def forward(spectral):
        coeffs = analysis(spectral)
        products = einsum("lkrc,wco->lkrwo", coeffs, weights)
        real = products[:, :, 0, 0] - products[:, :, 1, 1]
        imag = products[:, :, 0, 1] + products[:, :, 1, 0]
        mixed = jnp.stack([real, imag], axis=2) * spec_gain[:, None, None, :]
        return lax.all_gather(synthesis(mixed), "chan", axis=2, tiled=True)

    def backward(part):
        shaped = part.reshape(part.shape[0], part.shape[1], chans, chan_width)
        pieces = lax.all_to_all(shaped, "chan", split_axis=2, concat_axis=2, tiled=True)
        spectral = jnp.sum(pieces.astype(F32), axis=2).astype(BF)
        coeffs = analysis(spectral)
        scaled = (coeffs.astype(F32) * spec_gain[:, None, None, :]).astype(BF)
        products = einsum("lkro,wco->lkrwc", scaled, weights)
        real = products[:, :, 0, 0] + products[:, :, 1, 1]
        imag = products[:, :, 1, 0] - products[:, :, 0, 1]
        return synthesis(jnp.stack([real, imag], axis=2))

    return forward, backward


def shards(
    state,
    cotangent,
    order_table,
    quad_weight,
    legendre,
    spec_gain,
    spectral_weight,
    mlp_in,
    mlp_out,
):
    lats, chan_width, lon_count = state.shape
    chans = lax.axis_size("chan")
    me = lax.axis_index("chan")
    lon_width = lon_count // chans
    table = transform_table(order_table, lon_count)
    paths = spread_paths if legendre.shape[0] % chans == 0 else shard_paths
    forward, backward = paths(legendre, spec_gain, spectral_weight, lats, chan_width)

    point_state = chan_swap(state, 2, 1)
    first, second = chan_rows(mlp_in, True), chan_rows(mlp_out, True)
    weighting = jnp.repeat(jnp.where(order_table == 0, 1.0, 2.0), 2).astype(BF)
    own_table = lax.dynamic_slice_in_dim(table, me * lon_width, lon_width, 0)
    inverse = (own_table * weighting[None, :]).T

    spectral = einsum("tcn,nj->tjc", state, table)
    spectral = (spectral * quad_weight[:, None, None]).astype(BF)
    synth = forward(spectral)
    output, point_grad, part = mlp(point_state, cotangent, synth, inverse, first, second)
    hidden_grad = chan_swap(point_grad, 1, 2)
    field = backward(part)
    field_grad = einsum("tjc,nj->tcn", field, table) * quad_weight[:, None, None]
    state_grad = (hidden_grad.astype(F32) + field_grad).astype(BF)
    return output, state_grad


def solution(mesh):
    placed = (
        P("space", "chan", None),
        P("space", None, "chan"),
        P(),
        P("space"),
        P("space", "chan", None),
        P("chan", None),
        P(),
        P("chan", None),
        P("chan", None),
    )
    return jax.shard_map(
        shards,
        mesh=mesh,
        in_specs=placed,
        out_specs=(P("space", None, "chan"), P("space", "chan", None)),
        check_vma=False,
    )
```

```python
import functools
import math

import jax
import jax.numpy as jnp
from jax import lax
from jax.experimental import pallas as pl
from jax.experimental.pallas import tpu as pltpu
from jax.sharding import PartitionSpec as P


BF = jnp.bfloat16
F32 = jnp.float32
BOTH = ("space", "chan")
ROOT = math.sqrt(2.0 / math.pi)


def transform_table(order_table, lon_count):
    points = lax.broadcasted_iota(jnp.int32, (lon_count, 2 * order_table.shape[0]), 0)
    column = lax.broadcasted_iota(jnp.int32, (lon_count, 2 * order_table.shape[0]), 1)
    phases = points * jnp.repeat(order_table, 2)[None, :] % lon_count
    angles = phases.astype(F32) * (2.0 * math.pi / lon_count)
    waves = jnp.where(column % 2 == 0, jnp.cos(angles), -jnp.sin(angles))
    return (waves * (1.0 / math.sqrt(lon_count))).astype(BF)


def chan_swap(values, split_axis, concat_axis):
    count = lax.axis_size("chan")
    me = lax.axis_index("chan")
    width = values.shape[split_axis] // count
    depth = values.shape[concat_axis]
    shape = list(values.shape)
    shape[split_axis] = width
    shape[concat_axis] = depth * count
    result = jnp.zeros(shape, values.dtype)
    for shift in range(count):
        piece = lax.dynamic_slice_in_dim(values, (me + shift) % count * width, width, split_axis)
        if shift:
            ring = [(i, (i + shift) % count) for i in range(count)]
            piece = lax.ppermute(piece, "chan", ring)
        source = (me - shift + count) % count
        result = lax.dynamic_update_slice_in_dim(result, piece, source * depth, concat_axis)
    return result


def chan_swap_early(values, split_axis, concat_axis, early):
    me = lax.axis_index("chan")
    width = values.shape[split_axis] // 2
    depth = values.shape[concat_axis]
    shape = list(values.shape)
    shape[split_axis] = width
    shape[concat_axis] = depth * 2
    own = lax.dynamic_slice_in_dim(values, me * width, width, split_axis)
    result = jnp.zeros(shape, values.dtype)
    result = lax.dynamic_update_slice_in_dim(result, own, me * depth, concat_axis)
    spans = ((0, early), (early, values.shape[0]))
    for low, high in spans:
        rows = lax.slice_in_dim(values, low, high, axis=0)
        piece = lax.dynamic_slice_in_dim(rows, (1 - me) * width, width, split_axis)
        piece = lax.ppermute(piece, "chan", [(0, 1), (1, 0)])
        start = [0] * values.ndim
        start[0], start[concat_axis] = low, (1 - me) * depth
        result = lax.dynamic_update_slice(result, piece, start)
    return result


def chan_rows(values, share):
    count = lax.axis_size("chan")
    me = lax.axis_index("chan")
    rows = values.shape[0]
    result = jnp.zeros((rows * count,) + values.shape[1:], values.dtype)
    result = lax.dynamic_update_slice_in_dim(result, values, me * rows, 0)
    space = lax.axis_size("space")
    share = share and space % 2 == 0
    parity = lax.axis_index("space") % 2
    part = rows // 2 if share else rows
    mine = lax.dynamic_slice_in_dim(values, parity * part, part, 0) if share else values
    for shift in range(1, count):
        ring = [(i, (i + shift) % count) for i in range(count)]
        source = (me - shift + count) % count
        piece = lax.ppermute(mine, "chan", ring)
        if share:
            other = lax.ppermute(piece, "space", [(i, i ^ 1) for i in range(space)])
            result = lax.dynamic_update_slice_in_dim(
                result, piece, source * rows + parity * part, 0
            )
            result = lax.dynamic_update_slice_in_dim(
                result, other, source * rows + (1 - parity) * part, 0
            )
        else:
            result = lax.dynamic_update_slice_in_dim(result, piece, source * rows, 0)
    return result


def dot(left, right, dims):
    return lax.dot_general(left, right, (dims, ((), ())), preferred_element_type=F32)


def pick(base, rows, first):
    lanes = lax.broadcasted_iota(jnp.int32, (base.shape[0], rows), 1)
    return jnp.where(lanes == base[:, :1] + first, 1.0, 0.0).astype(BF)


def mlp_kernel(
    regroup, state, cot, synth, table, base, place, first, first_t, second, second_t,
    out, grad, spec, parts,
):
    grid_table = table[...]
    step = pl.program_id(0)
    lats = pl.num_programs(0)
    if regroup:
        rows = pick(base[...], synth.shape[0], step * regroup)
        waves = dot(rows, synth[...], ((1,), (0,))).astype(BF)
    else:
        waves = synth[0]
    wave = dot(waves, grid_table, ((0,), (0,)))
    hidden = (state[0].astype(F32) + wave).astype(BF)
    pre = dot(first_t[...], hidden, ((1,), (0,)))
    square = pre * pre
    curve = jnp.tanh(ROOT * (pre + 0.044715 * (square * pre)))
    half = 0.5 * (1.0 + curve)
    active = (pre * half).astype(BF)
    out[0] = (hidden.astype(F32) + dot(second_t[...], active, ((1,), (0,)))).astype(BF)
    slope = half + 0.5 * pre * (1.0 - curve * curve) * (ROOT * (1.0 + 0.134145 * square))
    inner = (slope * dot(second[...], cot[0], ((1,), (0,)))).astype(BF)
    back = (cot[0].astype(F32) + dot(first[...], inner, ((1,), (0,)))).astype(BF)
    grad[0] = back
    part = dot(grid_table, back, ((1,), (1,))).astype(BF)
    if regroup:
        parts[step] = part

        @pl.when(step == lats - 1)
        def _():
            flat = parts[...].reshape(-1, part.shape[1])
            spec[...] = dot(place[...], flat, ((1,), (0,))).astype(BF)
    else:
        spec[0] = part


def whole(shape):
    return pl.BlockSpec(shape, lambda t: (0,) * len(shape))


def row(*shape):
    return pl.BlockSpec((1,) + shape, lambda t: (t, 0, 0))


def mlp(state, cot, synth, table, base, place, regroup, first, second):
    lats, chans, lons = state.shape
    waves = table.shape[0]
    operands = (table, base, place, first, first.T, second, second.T)
    wave_spec = whole(synth.shape) if regroup else row(waves, chans)
    wave_shape = synth.shape if regroup else (lats, waves, chans)
    return pl.pallas_call(
        functools.partial(mlp_kernel, regroup),
        grid=(lats,),
        in_specs=[row(chans, lons), row(chans, lons), wave_spec]
        + [whole(value.shape) for value in operands],
        out_specs=[row(chans, lons), row(chans, lons), wave_spec],
        out_shape=[
            jax.ShapeDtypeStruct((lats, chans, lons), BF),
            jax.ShapeDtypeStruct((lats, chans, lons), BF),
            jax.ShapeDtypeStruct(wave_shape, BF),
        ],
        scratch_shapes=[pltpu.VMEM((lats, waves, chans) if regroup else (1, 16, 128), BF)],
        compiler_params=pltpu.CompilerParams(vmem_limit_bytes=56 << 20),
    )(state, cot, synth, *operands)


def last_kernel(regroup, quad, hidden_grad, field, table, base, out):
    step = pl.program_id(0)
    rows = pick(base[...], field.shape[0], step * regroup)
    waves = dot(rows, field[...], ((1,), (0,))).astype(BF)
    wave = dot(waves, table[...], ((0,), (0,)))
    out[0] = (hidden_grad[0].astype(F32) + wave * quad[step]).astype(BF)


def last(quad, hidden_grad, field, table, base, regroup):
    lats, chans, lons = hidden_grad.shape
    return pl.pallas_call(
        functools.partial(last_kernel, regroup),
        grid=(lats,),
        in_specs=[pl.BlockSpec(memory_space=pltpu.SMEM), row(chans, lons)]
        + [whole(value.shape) for value in (field, table, base)],
        out_specs=row(chans, lons),
        out_shape=jax.ShapeDtypeStruct(hidden_grad.shape, BF),
        compiler_params=pltpu.CompilerParams(vmem_limit_bytes=40 << 20),
    )(quad, hidden_grad, field, table, base)


def expand(table, base, lines):
    slots = table.shape[0]
    return jnp.concatenate(
        [
            dot(table[k], pick(base, lines, 2 * k + r), ((1,), (0,))).astype(BF)
            for r in range(2)
            for k in range(slots)
        ],
        axis=0,
    )


def ahead_kernel(got, table, base, gain, weights, out):
    spaces, chans, rows, width = got.shape
    matrix = expand(table, base[...], spaces * rows)
    pieces = [got[:, y].reshape(spaces * rows, width) for y in range(chans)]
    coeffs = jnp.concatenate(
        [dot(matrix, piece, ((1,), (0,))).astype(BF) for piece in pieces], axis=1
    )
    count = coeffs.shape[0] // 2
    real, imag = coeffs[:count], coeffs[count:]
    left, right = weights[0], weights[1]
    flat = ((1,), (0,))
    gains = jnp.concatenate([gain[...]] * table.shape[0], axis=0)
    top = ((dot(real, left, flat) - dot(imag, right, flat)) * gains).astype(BF)
    low = ((dot(real, right, flat) + dot(imag, left, flat)) * gains).astype(BF)
    mixed = jnp.concatenate([top, low], axis=0)
    synth = dot(matrix, mixed, ((0,), (0,))).astype(BF).reshape(spaces, rows, -1)
    for y in range(chans):
        out[:, y] = synth


def behind_kernel(got, table, base, gain, weights, out):
    spaces, chans, rows, channels = got.shape
    matrix = expand(table, base[...], spaces * rows)
    total = None
    for y in range(chans):
        term = dot(matrix, got[:, y].reshape(spaces * rows, channels), ((1,), (0,)))
        total = term if total is None else total + term
    coeffs = total.astype(BF).astype(F32)
    count = coeffs.shape[0] // 2
    gains = jnp.concatenate([gain[...]] * table.shape[0], axis=0)
    real = (coeffs[:count] * gains).astype(BF)
    imag = (coeffs[count:] * gains).astype(BF)
    left, right = weights[0], weights[1]
    flat = ((1,), (1,))
    top = (dot(real, left, flat) + dot(imag, right, flat)).astype(BF)
    low = (dot(imag, left, flat) - dot(real, right, flat)).astype(BF)
    mixed = jnp.concatenate([top, low], axis=0)
    field = dot(matrix, mixed, ((0,), (0,))).astype(BF).reshape(spaces, rows, channels)
    width = channels // chans
    for y in range(chans):
        out[:, y] = field[:, :, y * width : (y + 1) * width]


def stage(kernel, got, table, base, gain, weights, width):
    return pl.pallas_call(
        kernel,
        out_shape=jax.ShapeDtypeStruct(got.shape[:3] + (width,), BF),
        compiler_params=pltpu.CompilerParams(vmem_limit_bytes=48 << 20),
    )(got, table, base, gain, weights)


def einsum(form, *values):
    return jnp.einsum(form, *values, preferred_element_type=F32)


def spread_paths(legendre, spec_gain, weights, lats, chan_width):
    spaces, chans = lax.axis_size("space"), lax.axis_size("chan")
    devices = spaces * chans
    table = chan_swap(legendre, 0, 1)
    slots, _, lat_count = table.shape
    gains = chan_rows(spec_gain, False)
    channels = weights.shape[1]
    lines = lats * slots * 2
    rows = -(-lines // 8) * 8
    lat = jnp.arange(lat_count, dtype=jnp.int32)
    spot = lat // lats * rows + lat % lats * (2 * slots)
    spot = jnp.broadcast_to(spot[:, None], (lat_count, 128))

    def swap(values):
        flat = values.reshape((devices,) + values.shape[-2:])
        return lax.all_to_all(flat, BOTH, 0, 0, tiled=True)

    def parted(values):
        return values.reshape((spaces, chans) + values.shape[1:])

    def forward(spectral):
        sent = spectral.reshape(lats, devices, 2 * slots, chan_width).transpose(1, 0, 2, 3)
        sent = sent.reshape(devices, lines, chan_width)
        sent = jnp.pad(sent, [(0, 0), (0, rows - lines), (0, 0)])
        got = swap(sent)
        synth = stage(ahead_kernel, parted(got), table, spot, gains, weights, channels)
        return swap(synth).reshape(devices * rows, channels)

    def backward(part):
        got = swap(part.reshape(devices, rows, channels))
        field = stage(behind_kernel, parted(got), table, spot, gains, weights, chan_width)
        return swap(field).reshape(devices * rows, chan_width)

    wave = jnp.arange(devices * slots * 2, dtype=jnp.int32)
    base = wave // (2 * slots) * rows + wave % (2 * slots)
    spots = base[None, :] + 2 * slots * jnp.arange(lats, dtype=jnp.int32)[:, None]
    lines_all = jnp.arange(devices * rows, dtype=jnp.int32)
    place = (lines_all[:, None] == spots.reshape(1, -1)).astype(BF)
    base = jnp.broadcast_to(base[:, None], (base.shape[0], 128))
    return forward, backward, base, place, 2 * slots


def shard_paths(legendre, spec_gain, weights, lats, chan_width):
    chans = lax.axis_size("chan")
    table = lax.all_gather(legendre, "chan", axis=1, tiled=True)

    def to_orders(values):
        return lax.all_to_all(values, "space", split_axis=1, concat_axis=0, tiled=True)

    def to_bands(values):
        return lax.all_to_all(values, "space", split_axis=0, concat_axis=1, tiled=True)

    def to_degrees(values):
        return lax.all_to_all(values, "chan", split_axis=0, concat_axis=3, tiled=True)

    def to_channels(values):
        return lax.all_to_all(values, "chan", split_axis=3, concat_axis=0, tiled=True)

    def analysis(spectral):
        values = spectral.reshape(lats, -1, 2, chan_width)
        coeffs = einsum("klt,tkrc->lkrc", table, to_orders(values)).astype(BF)
        return to_degrees(coeffs)

    def synthesis(mixed):
        field = einsum("klt,lkrc->tkrc", table, to_channels(mixed.astype(BF))).astype(BF)
        return to_bands(field).reshape(lats, -1, chan_width)

    def forward(spectral):
        coeffs = analysis(spectral)
        products = einsum("lkrc,wco->lkrwo", coeffs, weights)
        real = products[:, :, 0, 0] - products[:, :, 1, 1]
        imag = products[:, :, 0, 1] + products[:, :, 1, 0]
        mixed = jnp.stack([real, imag], axis=2) * spec_gain[:, None, None, :]
        return lax.all_gather(synthesis(mixed), "chan", axis=2, tiled=True)

    def backward(part):
        shaped = part.reshape(part.shape[0], part.shape[1], chans, chan_width)
        pieces = lax.all_to_all(shaped, "chan", split_axis=2, concat_axis=2, tiled=True)
        spectral = jnp.sum(pieces.astype(F32), axis=2).astype(BF)
        coeffs = analysis(spectral)
        scaled = (coeffs.astype(F32) * spec_gain[:, None, None, :]).astype(BF)
        products = einsum("lkro,wco->lkrwc", scaled, weights)
        real = products[:, :, 0, 0] + products[:, :, 1, 1]
        imag = products[:, :, 1, 0] - products[:, :, 0, 1]
        return synthesis(jnp.stack([real, imag], axis=2))

    nothing = jnp.zeros((8, 128), jnp.int32)
    return forward, backward, nothing, nothing.astype(BF), 0


def shards(
    state,
    cotangent,
    order_table,
    quad_weight,
    legendre,
    spec_gain,
    spectral_weight,
    mlp_in,
    mlp_out,
):
    lats, chan_width, lon_count = state.shape
    chans = lax.axis_size("chan")
    me = lax.axis_index("chan")
    lon_width = lon_count // chans
    table = transform_table(order_table, lon_count)
    paths = spread_paths if legendre.shape[0] % chans == 0 else shard_paths
    forward, backward, base, place, regroup = paths(
        legendre, spec_gain, spectral_weight, lats, chan_width
    )

    if chans == 2:
        point_state = chan_swap_early(state, 2, 1, lats // 3)
    else:
        point_state = chan_swap(state, 2, 1)
    first = chan_rows(mlp_in, True)
    second = chan_rows(mlp_out, True)
    weighting = jnp.repeat(jnp.where(order_table == 0, 1.0, 2.0), 2).astype(BF)
    own_table = lax.dynamic_slice_in_dim(table, me * lon_width, lon_width, 0)
    inverse = (own_table * weighting[None, :]).T

    spectral = einsum("tcn,nj->tjc", state, table)
    spectral = (spectral * quad_weight[:, None, None]).astype(BF)
    synth = forward(spectral)
    output, point_grad, part = mlp(
        point_state, cotangent, synth, inverse, base, place, regroup, first, second
    )
    hidden_grad = chan_swap(point_grad, 1, 2)
    field = backward(part)
    if regroup:
        return output, last(quad_weight, hidden_grad, field, table.T, base, regroup)
    field_grad = einsum("tjc,nj->tcn", field, table) * quad_weight[:, None, None]
    return output, (hidden_grad.astype(F32) + field_grad).astype(BF)


def solution(mesh):
    placed = (
        P("space", "chan", None),
        P("space", None, "chan"),
        P(),
        P("space"),
        P("space", "chan", None),
        P("chan", None),
        P(),
        P("chan", None),
        P("chan", None),
    )
    return jax.shard_map(
        shards,
        mesh=mesh,
        in_specs=placed,
        out_specs=(P("space", None, "chan"), P("space", "chan", None)),
        check_vma=False,
    )
```
